32 devices in a mesh: long: 16 (over z, y, x), short: 2 (over core).
Axes of the slice: x: 2, y: 2, z: 4, core: 2. Of those that a mesh axis runs over, the one named last changes fastest.
Arguments:
- outer_block: bfloat16 [2, 16, 2, 512, 512], P('short', 'long'), may hold values from -0.15625 to 0.15625
- outflow_block: bfloat16 [2, 16, 2, 512, 512], P('short', 'long'), may hold values from -0.15625 to 0.15625
- inflow_block: bfloat16 [2, 16, 2, 512, 512], P('short', 'long'), may hold values from -0.15625 to 0.15625
- shared_block: bfloat16 [2, 16, 2, 512, 512], P('short', 'long'), may hold values from -1 to 1
Outputs:
- own_block: float32 [2, 2, 512, 4096], P('short', None, None, 'long')
- cross_block: float32 [2, 2, 512, 4096], P('short', None, None, 'long')
The draws below stay inside these ranges and needn't reach their ends.
All inputs are finite; a program needn't handle non-finite values.
Results may differ from the reference program's by a relative error of at most 0.0095.
Values may be sent and summed in bfloat16 or wider, within the bound.
No kernel may reach another device: no remote copies, remote signals or barrier semaphores. Data moves between devices by JAX's collectives and lax.ppermute only.
A program may use at most 64 MiB of HBM per device.

```python
import math
import jax
import jax.numpy as jnp
from jax import lax

N_IF = 512
TERMS = 3
N_LONG = 16
N_SHORT = 2


def draw_shared_block(key, part):
    first_key, second_key = jax.random.split(jax.random.fold_in(key, 17))
    full_shape = (N_SHORT, N_LONG, 2, N_IF, N_IF)
    spread = 0.15 / math.sqrt(2.0 * N_IF)
    diagonal = jax.random.uniform(first_key, (N_SHORT, N_LONG, N_IF), jnp.float32, 0.3, 0.7)
    jitter = jax.random.normal(second_key, full_shape, jnp.float32) * spread
    row_index = lax.broadcasted_iota(jnp.int32, (N_IF, N_IF), 0)
    column_index = lax.broadcasted_iota(jnp.int32, (N_IF, N_IF), 1)
    identity = (row_index == column_index).astype(jnp.float32)
    real_part = diagonal[:, :, :, None] * identity
    stacked = jnp.stack([real_part, jnp.zeros_like(real_part)], axis=2)
    return (jitter + stacked).astype(jnp.bfloat16)


def steps_of(rng, shape, shards, low, high):
    def one(position, parts):
        steps = jax.random.uniform(jax.random.fold_in(jax.random.fold_in(rng, 6), position), (parts,), jnp.float32, low / len(shards), high / len(shards))
        return jnp.repeat(jnp.exp(steps), shape[position] // parts).reshape((-1,) + (1,) * (len(shape) - position - 1))

    gain = one(*shards[0])
    for cut in shards[1:]:
        gain = gain * one(*cut)
    return gain


def noise(stream_key, dims, deviation, bound, shards=(), held_as=jnp.bfloat16):
    array = jax.random.normal(stream_key, dims, jnp.float32) * deviation
    if len(shards) > 0:
        array = steps_of(stream_key, dims, shards, -0.22, 0.18) * array
    return jnp.clip(array, min=-bound, max=bound).astype(held_as)


def setup_inputs(seed: int = 0) -> dict:
    key_of = jax.random.split(jax.random.key(seed), 5)
    outer_block = noise(key_of[0], (N_SHORT, N_LONG, 2, N_IF, N_IF), (25 * N_IF // 8) ** -0.5, 0.15625, ((0, 2), (1, 16)))
    outflow_block = noise(key_of[1], (N_SHORT, N_LONG, 2, N_IF, N_IF), (25 * N_IF // 8) ** -0.5, 0.15625, ((0, 2), (1, 16)))
    inflow_block = noise(key_of[2], (N_SHORT, N_LONG, 2, N_IF, N_IF), (25 * N_IF // 8) ** -0.5, 0.15625, ((0, 2), (1, 16)))
    shared_block = draw_shared_block(jax.random.fold_in(key_of[4], 71), 0)
    return {"outer_block": outer_block, "outflow_block": outflow_block, "inflow_block": inflow_block, "shared_block": shared_block}


def complex_product(left_matrix, right_matrix):
    left_real = left_matrix[0].astype(jnp.float32)
    left_imag = left_matrix[1].astype(jnp.float32)
    right_real = right_matrix[0].astype(jnp.float32)
    right_imag = right_matrix[1].astype(jnp.float32)
    highest = lax.Precision.HIGHEST
    real_part = jnp.dot(left_real, right_real, precision=highest) - jnp.dot(left_imag, right_imag, precision=highest)
    imag_part = jnp.dot(left_real, right_imag, precision=highest) + jnp.dot(left_imag, right_real, precision=highest)
    return jnp.stack([real_part, imag_part])

def merge_pair(corner_self, corner_peer, inflow_self, outer_self, outflow_self, outflow_peer):
    product = complex_product(corner_self, corner_peer).astype(jnp.bfloat16)
    start_value = inflow_self.astype(jnp.float32)
    current = start_value
    for iteration in range(TERMS - 1):
        current = start_value + complex_product(product, current.astype(jnp.bfloat16))
    series = current.astype(jnp.bfloat16)
    mapped = complex_product(corner_peer, series).astype(jnp.bfloat16)
    diagonal_part = outer_self.astype(jnp.float32) + complex_product(outflow_self, mapped)
    cross_part = complex_product(outflow_peer, series)
    return (diagonal_part, cross_part)

def reference(outer_block, outflow_block, inflow_block, shared_block):

    def first_level(leaf_index):
        row_index = leaf_index // N_LONG
        column_index = leaf_index % N_LONG
        partner = column_index + 1 - 2 * (column_index % 2)
        diagonal_part, cross_part = merge_pair(shared_block[row_index, column_index], shared_block[row_index, partner], inflow_block[row_index, column_index], outer_block[row_index, column_index], outflow_block[row_index, column_index], outflow_block[row_index, partner])
        return (diagonal_part.astype(jnp.bfloat16), cross_part.astype(jnp.bfloat16))
    first_diag, first_cross = lax.map(first_level, jnp.arange(N_SHORT * N_LONG, dtype=jnp.int32))
    first_diag = first_diag.reshape((N_SHORT, N_LONG, 2, N_IF, N_IF))
    first_cross = first_cross.reshape((N_SHORT, N_LONG, 2, N_IF, N_IF))
    pair_count = N_LONG // 2

    def second_level(parent_index):
        row_index = parent_index // pair_count
        pair_index = parent_index % pair_count
        other_row = 1 - row_index
        left_leaf = 2 * pair_index
        right_leaf = left_leaf + 1
        diagonal_part, cross_part = merge_pair(first_diag[row_index, left_leaf], first_diag[other_row, left_leaf], first_cross[row_index, right_leaf], first_diag[row_index, right_leaf], first_cross[row_index, left_leaf], first_cross[other_row, left_leaf])
        factor = math.sqrt(N_IF)
        return (factor * diagonal_part, factor * cross_part)
    own_parts, cross_parts = lax.map(second_level, jnp.arange(N_SHORT * pair_count, dtype=jnp.int32))

    def arrange(blocks):
        blocks = blocks.reshape((N_SHORT, pair_count, 2, N_IF, N_IF))
        return blocks.transpose(0, 2, 3, 1, 4).reshape((N_SHORT, 2, N_IF, pair_count * N_IF))
    return (arrange(own_parts), arrange(cross_parts))
```

```python
import math

import jax
import jax.numpy as jnp
from jax import lax
from jax.sharding import PartitionSpec as P

TERMS = 3


def across(x, axis, parity):
    return lax.ppermute(x, axis, [(i, i ^ 1) for i in range(lax.axis_size(axis)) if i % 2 == parity])


def swap(x, axis):
    return lax.ppermute(x, axis, [(i, i ^ 1) for i in range(lax.axis_size(axis))])


def cdot(left, right):
    upper = jnp.concatenate([left[0], -left[1]], axis=1)
    lower = jnp.concatenate([left[1], left[0]], axis=1)
    stacked = jnp.concatenate([upper, lower], axis=0)
    column = jnp.concatenate([right[0], right[1]], axis=0)
    result = jnp.dot(stacked, column, preferred_element_type=jnp.float32)
    rows = left.shape[1]
    return jnp.stack([result[:rows], result[rows:]])


def rb(x):
    return x.astype(jnp.bfloat16)


def wide(x):
    return x.astype(jnp.float32)


def shards(outer_block, outflow_block, inflow_block, shared_block):
    outer, outflow, inflow, shared = outer_block[0, 0], outflow_block[0, 0], inflow_block[0, 0], shared_block[0, 0]
    width = outer.shape[2]
    half = width // 2
    is_left = lax.axis_index("long") % 2 == 0
    factor = math.sqrt(width)

    shared_r = across(shared, "long", 1)
    inflow_r1 = across(inflow[:, :, half:], "long", 1)
    inflow_r0 = across(inflow[:, :, :half], "long", 1)
    outflow_r = across(outflow, "long", 1)
    outer_r0 = across(outer[:, :, :half], "long", 1)

    product = rb(cdot(shared, shared_r))
    start = wide(inflow)
    series = rb(start + cdot(product, rb(start + cdot(product, inflow))))
    mapped = rb(cdot(shared_r, series))
    diag = rb(wide(outer) + cdot(outflow, mapped))
    diag_far = swap(diag, "short")
    series_far = swap(series, "short")
    product_two = rb(cdot(diag, diag_far))

    def columns(g):
        k = cdot(shared, g)
        kb = rb(k)
        v1 = rb(k + cdot(product, kb))
        shared_series = k + cdot(product, v1)
        right_series = rb(wide(g) + cdot(shared_r, v1))
        cross = rb(cdot(outflow, right_series))
        start_two = wide(cross)
        w = rb(start_two + cdot(product_two, rb(start_two + cdot(product_two, cross))))
        z = rb(cdot(diag_far, w))
        return rb(shared_series + cdot(series, z)), rb(cdot(series_far, w))

    x1, y1 = columns(inflow_r1)
    x1_r = across(x1, "long", 0)
    y1_r = across(y1, "long", 0)
    x0, y0 = columns(inflow_r0)

    outflow_b = jnp.where(is_left, outflow_r, outflow)
    outflow_b_far = swap(outflow_b, "short")
    x = jnp.where(is_left, x0, x1_r)
    y = jnp.where(is_left, y0, y1_r)
    outer_b = jnp.where(is_left, outer_r0, outer[:, :, half:])
    own = factor * (wide(outer_b) + cdot(outflow_b, x))
    far = factor * cdot(outflow_b_far, y)
    return own[None], far[None]


def solution(mesh):
    spec = P("short", "long", None, None, None)
    out = P("short", None, None, "long")
    return jax.shard_map(shards, mesh=mesh, in_specs=(spec,) * 4, out_specs=(out, out), check_vma=False)
```

```python
import functools
import math

import jax
import jax.numpy as jnp
from jax import lax
from jax.experimental import pallas as pl
from jax.experimental.pallas import tpu as pltpu
from jax.sharding import PartitionSpec as P


BF = jnp.bfloat16
F32 = jnp.float32


def across(x, axis, parity):
    return lax.ppermute(x, axis, [(i, i ^ 1) for i in range(lax.axis_size(axis)) if i % 2 == parity])


def swap(x, axis):
    return lax.ppermute(x, axis, [(i, i ^ 1) for i in range(lax.axis_size(axis))])


def cstage(left, right, emit, rows=256):
    n, k = left.shape[1], left.shape[2]
    m = right.shape[2]

    def body(i, carry):
        r = pl.ds(pl.multiple_of(i * rows, rows), rows)
        re, im = left[0, r, :], left[1, r, :]
        top = jnp.concatenate([re, -im], axis=1)
        bottom = jnp.concatenate([im, re], axis=1)
        lhs = jnp.concatenate([top, bottom], axis=0)
        out = jnp.dot(lhs, right[...].reshape(2 * k, m), preferred_element_type=F32)
        emit(r, out[:rows], out[rows:])
        return carry

    lax.fori_loop(0, n // rows, body, 0)


def plain(dst):
    def emit(r, re, im):
        dst[0, r, :] = re.astype(dst.dtype)
        dst[1, r, :] = im.astype(dst.dtype)

    return emit


def plus(dst, base):
    def emit(r, re, im):
        dst[0, r, :] = (base[0, r, :].astype(F32) + re).astype(dst.dtype)
        dst[1, r, :] = (base[1, r, :].astype(F32) + im).astype(dst.dtype)

    return emit


def level_one(t, h, hr, g, f, e, p, s, d, v, m):
    cstage(h, hr, plain(p))
    cstage(p, g, plus(v, g))
    cstage(p, v, plus(s, g))
    cstage(hr, s, plain(m))
    cstage(f, m, plus(d, e))


def gate(x, t):
    t[...] = x[...]


def second_product(d, df, q):
    cstage(d, df, plain(q))


def columns(h, hr, p, f, g, q, df, s, sf, xy, k32, kb, v1, sb, c, w1, w, z):
    def emit_k(r, re, im):
        k32[0, r, :] = re
        k32[1, r, :] = im
        kb[0, r, :] = re.astype(BF)
        kb[1, r, :] = im.astype(BF)

    cstage(h, g, emit_k)
    cstage(p, kb, plus(v1, k32))
    cstage(hr, v1, plus(sb, g))
    cstage(p, v1, plus(k32, k32))
    cstage(f, sb, plain(c))
    cstage(q, c, plus(w1, c))
    cstage(q, w1, plus(w, c))
    cstage(df, w, plain(z))
    cstage(s, z, plus(xy.at[0], k32))
    cstage(sf, w, plain(xy.at[1]))


def last(factor, f, ff, xy, own, far):
    def scaled(dst):
        def emit(r, re, im):
            dst[0, r, :] = re * factor
            dst[1, r, :] = im * factor

        return emit

    cstage(f, xy.at[0], scaled(own))
    cstage(ff, xy.at[1], scaled(far))


def call(body, outs, args, units, scratch=()):
    n = args[-1].shape[1]
    return pl.pallas_call(
        body,
        out_shape=[jax.ShapeDtypeStruct(s, t) for s, t in outs],
        in_specs=[pl.BlockSpec(memory_space=pltpu.VMEM)] * len(args),
        out_specs=[pl.BlockSpec(memory_space=pltpu.VMEM)] * len(outs),
        scratch_shapes=[pltpu.VMEM(s, t) for s, t in scratch],
        cost_estimate=pl.CostEstimate(
            flops=int(8 * n * n * n * units), bytes_accessed=4 * n * n * (len(args) + len(outs)), transcendentals=0
        ),
    )(*args)


def shards(outer_block, outflow_block, inflow_block, shared_block):
    outer, outflow, inflow, shared = outer_block[0, 0], outflow_block[0, 0], inflow_block[0, 0], shared_block[0, 0]
    n = outer.shape[2]
    half = n // 2
    is_left = lax.axis_index("long") % 2 == 0
    factor = math.sqrt(n)
    full, part = (2, n, n), (2, n, half)

    shared_r = across(shared, "long", 1)
    inflow_r1 = across(inflow[:, :, half:], "long", 1)
    inflow_r0 = across(inflow[:, :, :half], "long", 1)
    outflow_r = across(outflow, "long", 1)
    outer_r0 = across(outer[:, :, :half], "long", 1)

    token = pl.pallas_call(
        gate,
        grid=(1,),
        out_shape=jax.ShapeDtypeStruct((1, 16, 128), BF),
        in_specs=[pl.BlockSpec((1, 16, 128), lambda i: (0, 0, 0))],
        out_specs=pl.BlockSpec((1, 16, 128), lambda i: (0, 0, 0)),
        name="gate",
    )(outer)
    product, series, diag = call(
        level_one, [(full, BF)] * 3, (token, shared, shared_r, inflow, outflow, outer), 5, [(full, BF)] * 2
    )
    diag_far = swap(diag, "short")
    series_far = swap(series, "short")
    (product_two,) = call(second_product, [(full, BF)], (diag, diag_far), 1)

    def half_columns(g):
        return call(
            columns,
            [((2,) + part, BF)],
            (shared, shared_r, product, outflow, g, product_two, diag_far, series, series_far),
            5,
            [(part, F32)] + [(part, BF)] * 7,
        )[0]

    xy1 = half_columns(inflow_r1)
    xy1_r = across(xy1, "long", 0)
    xy0 = half_columns(inflow_r0)

    outflow_b = jnp.where(is_left, outflow_r, outflow)
    outflow_b_far = swap(outflow_b, "short")
    xy = jnp.where(is_left, xy0, xy1_r)
    own, far = call(functools.partial(last, factor), [(part, F32)] * 2, (outflow_b, outflow_b_far, xy), 1)
    outer_b = jnp.where(is_left, outer_r0, outer[:, :, half:])
    own = own + factor * outer_b.astype(F32)
    return own[None], far[None]


def solution(mesh):
    spec = P("short", "long", None, None, None)
    out = P("short", None, None, "long")
    return jax.shard_map(shards, mesh=mesh, in_specs=(spec,) * 4, out_specs=(out, out), check_vma=False)
```

```python
import functools
import math

import jax
import jax.numpy as jnp
from jax import lax
from jax.experimental import pallas as pl
from jax.experimental.pallas import tpu as pltpu
from jax.sharding import PartitionSpec as P


BF = jnp.bfloat16
F32 = jnp.float32


def across(x, axis, parity):
    return lax.ppermute(x, axis, [(i, i ^ 1) for i in range(lax.axis_size(axis)) if i % 2 == parity])


def swap(x, axis):
    return lax.ppermute(x, axis, [(i, i ^ 1) for i in range(lax.axis_size(axis))])


def cstage(left, right, emit):
    k, m = right.shape[1], right.shape[2]
    re, im = left[0], left[1]
    column = right[...].reshape(2 * k, m)
    upper = jnp.dot(jnp.concatenate([re, -im], axis=1), column, preferred_element_type=F32)
    lower = jnp.dot(jnp.concatenate([im, re], axis=1), column, preferred_element_type=F32)
    emit(upper, lower)


def cstage_two(left, right, left_b, right_b, emit):
    k, m = right.shape[1], right.shape[2]
    column, column_b = right[...].reshape(2 * k, m), right_b[...].reshape(2 * k, m)
    upper = jnp.dot(jnp.concatenate([left[0], -left[1]], axis=1), column, preferred_element_type=F32)
    upper += jnp.dot(jnp.concatenate([left_b[0], -left_b[1]], axis=1), column_b, preferred_element_type=F32)
    lower = jnp.dot(jnp.concatenate([left[1], left[0]], axis=1), column, preferred_element_type=F32)
    lower += jnp.dot(jnp.concatenate([left_b[1], left_b[0]], axis=1), column_b, preferred_element_type=F32)
    emit(upper, lower)


def plain(dst):
    def emit(re, im):
        dst[0] = re.astype(dst.dtype)
        dst[1] = im.astype(dst.dtype)

    return emit


def plus(dst, base):
    def emit(re, im):
        dst[0] = (base[0].astype(F32) + re).astype(dst.dtype)
        dst[1] = (base[1].astype(F32) + im).astype(dst.dtype)

    return emit


def level_one(t, h, hr, g, f, e, p, s, d, v, m):
    cstage(h, hr, plain(p))
    cstage(p, g, plus(v, g))
    cstage(p, v, plus(s, g))
    cstage(hr, s, plain(m))
    cstage(f, m, plus(d, e))


def gate(x, t):
    t[...] = x[...]


def second_product(d, df, q):
    cstage(d, df, plain(q))


def columns(h, hr, p, f, g, q, df, s, sf, xy, k32, kb, v1, sb, c, w1, w, z):
    def emit_k(re, im):
        k32[0], k32[1] = re, im
        kb[0], kb[1] = re.astype(BF), im.astype(BF)

    cstage(h, g, emit_k)
    cstage(p, kb, plus(v1, k32))
    cstage(hr, v1, plus(sb, g))
    cstage(f, sb, plain(c))
    cstage(q, c, plus(w1, c))
    cstage(q, w1, plus(w, c))
    cstage(df, w, plain(z))
    cstage_two(p, v1, s, z, plus(xy.at[0], k32))
    cstage(sf, w, plain(xy.at[1]))


def last(factor, flag, f_l, ff_l, xy_l, f_r, ff_r, xy_r, e_r, own, far, f, ff, xy, e, sems):
    def fetch(sources):
        copies = [pltpu.make_async_copy(a, b, sems.at[i]) for i, (a, b) in enumerate(sources)]
        for c in copies:
            c.start()
        for c in copies:
            c.wait()

    half = e.shape[2]

    @pl.when(flag[0] == 1)
    def _():
        fetch([(f_l, f), (ff_l, ff), (xy_l, xy)])
        e[...] = jnp.zeros_like(e)

    @pl.when(flag[0] == 0)
    def _():
        fetch([(f_r, f), (ff_r, ff), (xy_r, xy), (e_r.at[:, :, pl.ds(half, half)], e)])

    def scaled(dst, base=None):
        def emit(re, im):
            if base is not None:
                re, im = base[0].astype(F32) + re, base[1].astype(F32) + im
            dst[0], dst[1] = re * factor, im * factor

        return emit

    cstage(f, xy.at[0], scaled(own, e))
    cstage(ff, xy.at[1], scaled(far))


def finish(factor, own, e, out, buf, sems):
    rows = own.shape[1] // 2
    copies = []
    for c in range(2):
        for i in range(2):
            r = pl.ds(i * rows, rows)
            buf[c, r, :] = own[c, r, :] + e[c, r, :].astype(F32) * factor
            copies.append(pltpu.make_async_copy(buf.at[c, r, :], out.at[c, r, :], sems.at[2 * c + i]))
            copies[-1].start()
    for c in copies:
        c.wait()


def call(body, outs, args, units, scratch=(), specs=None, out_spec=None):
    n = args[-1].shape[1]
    vmem = pl.BlockSpec(memory_space=pltpu.VMEM)
    return pl.pallas_call(
        body,
        out_shape=[jax.ShapeDtypeStruct(s, t) for s, t in outs],
        in_specs=specs or [vmem] * len(args),
        out_specs=[out_spec or vmem] * len(outs),
        scratch_shapes=[pltpu.VMEM(*s) if isinstance(s, tuple) else s for s in scratch],
        cost_estimate=pl.CostEstimate(
            flops=int(8 * n * n * n * units),
            bytes_accessed=4 * n * n * (len(args) + len(outs)),
            transcendentals=0,
        ),
        compiler_params=pltpu.CompilerParams(vmem_limit_bytes=24 << 20),
    )(*args)


def shards(outer_block, outflow_block, inflow_block, shared_block):
    outer, outflow, inflow, shared = outer_block[0, 0], outflow_block[0, 0], inflow_block[0, 0], shared_block[0, 0]
    n = outer.shape[2]
    half = n // 2
    factor = math.sqrt(n)
    full, part = (2, n, n), (2, n, half)

    shared_r = across(shared, "long", 1)
    inflow_r1 = across(inflow[:, :, half:], "long", 1)
    inflow_r0 = across(inflow[:, :, :half], "long", 1)
    outflow_r = across(outflow, "long", 1)
    outer_r0 = across(outer[:, :, :half], "long", 1)
    outflow_far = swap(outflow, "short")

    token = pl.pallas_call(
        gate,
        grid=(1,),
        out_shape=jax.ShapeDtypeStruct((1, 16, 128), BF),
        in_specs=[pl.BlockSpec((1, 16, 128), lambda i: (0, 0, 0))],
        out_specs=pl.BlockSpec((1, 16, 128), lambda i: (0, 0, 0)),
        name="gate",
    )(outer)
    product, series, diag = call(
        level_one, [(full, BF)] * 3, (token, shared, shared_r, inflow, outflow, outer), 5, [(full, BF)] * 2
    )
    diag_far = swap(diag, "short")
    series_far = swap(series, "short")
    (product_two,) = call(second_product, [(full, BF)], (diag, diag_far), 1)

    def half_columns(g):
        return call(
            columns,
            [((2,) + part, BF)],
            (shared, shared_r, product, outflow, g, product_two, diag_far, series, series_far),
            5,
            [(part, F32)] + [(part, BF)] * 7,
        )[0]

    xy1 = half_columns(inflow_r1)
    xy1_r = across(xy1, "long", 0)
    xy0 = half_columns(inflow_r0)

    outflow_r_far = swap(outflow_r, "short")
    flag = (lax.axis_index("long") % 2 == 0).astype(jnp.int32).reshape(1)
    hbm = pl.BlockSpec(memory_space=pltpu.HBM)
    own, far = call(
        functools.partial(last, factor),
        [(part, F32)] * 2,
        (flag, outflow_r, outflow_r_far, xy0, outflow, outflow_far, xy1_r, outer),
        1,
        [(full, BF), (full, BF), ((2,) + part, BF), (part, BF), pltpu.SemaphoreType.DMA((4,))],
        [pl.BlockSpec(memory_space=pltpu.SMEM)] + [hbm] * 7,
    )
    (own,) = call(
        functools.partial(finish, factor),
        [(part, F32)],
        (own, outer_r0),
        0,
        [(part, F32), pltpu.SemaphoreType.DMA((4,))],
        None,
        hbm,
    )
    return own[None], far[None]


def solution(mesh):
    spec = P("short", "long", None, None, None)
    out = P("short", None, None, "long")
    return jax.shard_map(shards, mesh=mesh, in_specs=(spec,) * 4, out_specs=(out, out), check_vma=False)
```

```python
import functools
import math

import jax
import jax.numpy as jnp
from jax import lax
from jax.experimental import pallas as pl
from jax.experimental.pallas import tpu as pltpu
from jax.sharding import PartitionSpec as P


BF = jnp.bfloat16
F32 = jnp.float32


def across(x, axis, parity):
    return lax.ppermute(x, axis, [(i, i ^ 1) for i in range(lax.axis_size(axis)) if i % 2 == parity])


def swap(x, axis):
    return lax.ppermute(x, axis, [(i, i ^ 1) for i in range(lax.axis_size(axis))])


def cstage(left, right, emit):
    k, m = right.shape[1], right.shape[2]
    re, im = left[0], left[1]
    column = right[...].reshape(2 * k, m)
    upper = jnp.dot(jnp.concatenate([re, -im], axis=1), column, preferred_element_type=F32)
    lower = jnp.dot(jnp.concatenate([im, re], axis=1), column, preferred_element_type=F32)
    emit(upper, lower)


def cstage_two(left, right, left_b, right_b, emit):
    k, m = right.shape[1], right.shape[2]
    column, column_b = right[...].reshape(2 * k, m), right_b[...].reshape(2 * k, m)
    upper = jnp.dot(jnp.concatenate([left[0], -left[1]], axis=1), column, preferred_element_type=F32)
    upper += jnp.dot(jnp.concatenate([left_b[0], -left_b[1]], axis=1), column_b, preferred_element_type=F32)
    lower = jnp.dot(jnp.concatenate([left[1], left[0]], axis=1), column, preferred_element_type=F32)
    lower += jnp.dot(jnp.concatenate([left_b[1], left_b[0]], axis=1), column_b, preferred_element_type=F32)
    emit(upper, lower)


def plain(dst):
    def emit(re, im):
        dst[0] = re.astype(dst.dtype)
        dst[1] = im.astype(dst.dtype)

    return emit


def plus(dst, base):
    def emit(re, im):
        dst[0] = (base[0].astype(F32) + re).astype(dst.dtype)
        dst[1] = (base[1].astype(F32) + im).astype(dst.dtype)

    return emit


def level_one(t, h, hr, g, f, e, p, s, d, v, m):
    cstage(h, hr, plain(p))
    cstage(p, g, plus(v, g))
    cstage(p, v, plus(s, g))
    cstage(hr, s, plain(m))
    cstage(f, m, plus(d, e))


def gate(x, t):
    t[...] = x[...]


def second_product(d, df, q):
    cstage(d, df, plain(q))


def columns(h, hr, p, f, g, q, df, s, sf, xy, k32, kb, v1, sb, c, w1, w, z):
    def emit_k(re, im):
        k32[0], k32[1] = re, im
        kb[0], kb[1] = re.astype(BF), im.astype(BF)

    cstage(h, g, emit_k)
    cstage(p, kb, plus(v1, k32))
    cstage(hr, v1, plus(sb, g))
    cstage(f, sb, plain(c))
    cstage(q, c, plus(w1, c))
    cstage(q, w1, plus(w, c))
    cstage(df, w, plain(z))
    cstage_two(p, v1, s, z, plus(xy.at[0], k32))
    cstage(sf, w, plain(xy.at[1]))


def last(factor, flag, f_l, ff_l, xy_l, f_r, ff_r, xy_r, e_r, own, far, f, ff, xy, e, sems):
    def fetch(sources):
        copies = [pltpu.make_async_copy(a, b, sems.at[i]) for i, (a, b) in enumerate(sources)]
        for c in copies:
            c.start()
        for c in copies:
            c.wait()

    half = e.shape[2]

    @pl.when(flag[0] == 1)
    def _():
        fetch([(f_l, f), (ff_l, ff), (xy_l, xy)])
        e[...] = jnp.zeros_like(e)

    @pl.when(flag[0] == 0)
    def _():
        fetch([(f_r, f), (ff_r, ff), (xy_r, xy), (e_r.at[:, :, pl.ds(half, half)], e)])

    def scaled(dst, base=None):
        def emit(re, im):
            if base is not None:
                re, im = base[0].astype(F32) + re, base[1].astype(F32) + im
            dst[0], dst[1] = re * factor, im * factor

        return emit

    cstage(f, xy.at[0], scaled(own, e))
    cstage(ff, xy.at[1], scaled(far))


def finish(factor, first, own, e, *rest):
    out, buf, sems = rest[-3:]
    copies = []
    for c in range(2):
        r = pl.ds(first, e.shape[1])
        buf[c] = own[c, r, :] + e[c].astype(F32) * factor
        copies.append(pltpu.make_async_copy(buf.at[c], out.at[c, r, :], sems.at[c]))
        copies[-1].start()
    for c in copies:
        c.wait()


def call(body, outs, args, units, scratch=(), specs=None, out_spec=None, aliases=None):
    n = args[-1].shape[1] if units else 0
    vmem = pl.BlockSpec(memory_space=pltpu.VMEM)
    return pl.pallas_call(
        body,
        out_shape=[jax.ShapeDtypeStruct(s, t) for s, t in outs],
        in_specs=specs or [vmem] * len(args),
        out_specs=[out_spec or vmem] * len(outs),
        scratch_shapes=[pltpu.VMEM(*s) if isinstance(s, tuple) else s for s in scratch],
        cost_estimate=pl.CostEstimate(
            flops=int(8 * n * n * n * units),
            bytes_accessed=4 * n * n * (len(args) + len(outs)),
            transcendentals=0,
        ),
        compiler_params=pltpu.CompilerParams(vmem_limit_bytes=24 << 20),
        input_output_aliases=aliases or {},
    )(*args)


def shards(outer_block, outflow_block, inflow_block, shared_block):
    outer, outflow, inflow, shared = outer_block[0, 0], outflow_block[0, 0], inflow_block[0, 0], shared_block[0, 0]
    n = outer.shape[2]
    half = n // 2
    factor = math.sqrt(n)
    full, part = (2, n, n), (2, n, half)

    shared_r = across(shared, "long", 1)
    inflow_r1 = across(inflow[:, :, half:], "long", 1)
    inflow_r0 = across(inflow[:, :, :half], "long", 1)
    outflow_r = across(outflow, "long", 1)
    cut = n * 3 // 4
    outer_r0 = across(outer[:, :cut, :half], "long", 1)
    outer_r1 = across(outer[:, cut:, :half], "long", 1)
    outflow_far = swap(outflow, "short")

    token = pl.pallas_call(
        gate,
        grid=(1,),
        out_shape=jax.ShapeDtypeStruct((1, 16, 128), BF),
        in_specs=[pl.BlockSpec((1, 16, 128), lambda i: (0, 0, 0))],
        out_specs=pl.BlockSpec((1, 16, 128), lambda i: (0, 0, 0)),
        name="gate",
    )(outer)
    product, series, diag = call(
        level_one, [(full, BF)] * 3, (token, shared, shared_r, inflow, outflow, outer), 5, [(full, BF)] * 2
    )
    diag_far = swap(diag, "short")
    series_far = swap(series, "short")
    (product_two,) = call(second_product, [(full, BF)], (diag, diag_far), 1)

    def half_columns(g):
        return call(
            columns,
            [((2,) + part, BF)],
            (shared, shared_r, product, outflow, g, product_two, diag_far, series, series_far),
            5,
            [(part, F32)] + [(part, BF)] * 7,
        )[0]

    xy1 = half_columns(inflow_r1)
    xy1_r = across(xy1, "long", 0)
    xy0 = half_columns(inflow_r0)

    outflow_r_far = swap(outflow_r, "short")
    flag = (lax.axis_index("long") % 2 == 0).astype(jnp.int32).reshape(1)
    hbm = pl.BlockSpec(memory_space=pltpu.HBM)
    own, far = call(
        functools.partial(last, factor),
        [(part, F32)] * 2,
        (flag, outflow_r, outflow_r_far, xy0, outflow, outflow_far, xy1_r, outer),
        1,
        [(full, BF), (full, BF), ((2,) + part, BF), (part, BF), pltpu.SemaphoreType.DMA((4,))],
        [pl.BlockSpec(memory_space=pltpu.SMEM)] + [hbm] * 7,
    )

    def add(first, rows, *more):
        return call(
            functools.partial(finish, factor, first),
            [(part, F32)],
            (own,) + rows + more,
            0,
            [((2,) + rows[0].shape[1:], F32), pltpu.SemaphoreType.DMA((2,))],
            [pl.BlockSpec(memory_space=pltpu.VMEM)] * 2 + [hbm] * len(more),
            hbm,
            {2: 0} if more else None,
        )[0]

    partly = add(0, (outer_r0,))
    own = add(cut, (outer_r1,), partly)
    return own[None], far[None]


def solution(mesh):
    spec = P("short", "long", None, None, None)
    out = P("short", None, None, "long")
    return jax.shard_map(shards, mesh=mesh, in_specs=(spec,) * 4, out_specs=(out, out), check_vma=False)
```

```python
import functools
import math

import jax
import jax.numpy as jnp
from jax import lax
from jax.experimental import pallas as pl
from jax.experimental.pallas import tpu as pltpu
from jax.sharding import PartitionSpec as P


BF = jnp.bfloat16
F32 = jnp.float32


def across(x, axis, parity):
    return lax.ppermute(x, axis, [(i, i ^ 1) for i in range(lax.axis_size(axis)) if i % 2 == parity])


def swap(x, axis):
    return lax.ppermute(x, axis, [(i, i ^ 1) for i in range(lax.axis_size(axis))])


def cstage(left, right, emit):
    k, m = right.shape[1], right.shape[2]
    re, im = left[0], left[1]
    column = right[...].reshape(2 * k, m)
    upper = jnp.dot(jnp.concatenate([re, -im], axis=1), column, preferred_element_type=F32)
    lower = jnp.dot(jnp.concatenate([im, re], axis=1), column, preferred_element_type=F32)
    emit(upper, lower)


def cstage_two(left, right, left_b, right_b, emit):
    k, m = right.shape[1], right.shape[2]
    column, column_b = right[...].reshape(2 * k, m), right_b[...].reshape(2 * k, m)
    upper = jnp.dot(jnp.concatenate([left[0], -left[1]], axis=1), column, preferred_element_type=F32)
    upper += jnp.dot(jnp.concatenate([left_b[0], -left_b[1]], axis=1), column_b, preferred_element_type=F32)
    lower = jnp.dot(jnp.concatenate([left[1], left[0]], axis=1), column, preferred_element_type=F32)
    lower += jnp.dot(jnp.concatenate([left_b[1], left_b[0]], axis=1), column_b, preferred_element_type=F32)
    emit(upper, lower)


def plain(dst):
    def emit(re, im):
        dst[0] = re.astype(dst.dtype)
        dst[1] = im.astype(dst.dtype)

    return emit


def plus(dst, base):
    def emit(re, im):
        dst[0] = (base[0].astype(F32) + re).astype(dst.dtype)
        dst[1] = (base[1].astype(F32) + im).astype(dst.dtype)

    return emit


def level_one(t, h, hr, g, f, e, p, s, d, v, m):
    cstage(h, hr, plain(p))
    cstage(p, g, plus(v, g))
    cstage(p, v, plus(s, g))
    cstage(hr, s, plain(m))
    cstage(f, m, plus(d, e))


def gate(x, t):
    t[...] = x[...]


def second_product(d, df, q):
    cstage(d, df, plain(q))


def columns(h, hr, p, f, g, q, df, s, sf, xy, k32, kb, v1, sb, c, w1, w, z):
    def emit_k(re, im):
        k32[0], k32[1] = re, im
        kb[0], kb[1] = re.astype(BF), im.astype(BF)

    cstage(h, g, emit_k)
    cstage(p, kb, plus(v1, k32))
    cstage(hr, v1, plus(sb, g))
    cstage(f, sb, plain(c))
    cstage(q, c, plus(w1, c))
    cstage(q, w1, plus(w, c))
    cstage(df, w, plain(z))
    cstage_two(p, v1, s, z, plus(xy.at[0], k32))
    cstage(sf, w, plain(xy.at[1]))


def fetch(flag, left, right, sems):
    def run(pairs):
        copies = [pltpu.make_async_copy(a, b, sems.at[i]) for i, (a, b) in enumerate(pairs)]
        for c in copies:
            c.start()
        for c in copies:
            c.wait()

    @pl.when(flag[0] == 1)
    def _():
        run(left)

    @pl.when(flag[0] == 0)
    def _():
        run(right)


def last_own(factor, flag, f_l, xy_l, f_r, xy_r, e_r, own, f, x, e, sems):
    half = e.shape[2]
    e[...] = jnp.zeros_like(e)
    fetch(
        flag,
        [(f_l, f), (xy_l.at[0], x)],
        [(f_r, f), (xy_r.at[0], x), (e_r.at[:, :, pl.ds(half, half)], e)],
        sems,
    )

    def emit(re, im):
        own[0] = (e[0].astype(F32) + re) * factor
        own[1] = (e[1].astype(F32) + im) * factor

    cstage(f, x, emit)


def last_far(factor, flag, f_l, xy_l, f_r, xy_r, far, f, y, sems):
    fetch(flag, [(f_l, f), (xy_l.at[1], y)], [(f_r, f), (xy_r.at[1], y)], sems)

    def emit(re, im):
        far[0] = re * factor
        far[1] = im * factor

    cstage(f, y, emit)


def finish(factor, first, own, e, *rest):
    out, buf, sems = rest[-3:]
    copies = []
    for c in range(2):
        r = pl.ds(first, e.shape[1])
        buf[c] = own[c, r, :] + e[c].astype(F32) * factor
        copies.append(pltpu.make_async_copy(buf.at[c], out.at[c, r, :], sems.at[c]))
        copies[-1].start()
    for c in copies:
        c.wait()


def call(body, outs, args, units, scratch=(), specs=None, out_spec=None, aliases=None):
    n = args[1].shape[1]
    vmem = pl.BlockSpec(memory_space=pltpu.VMEM)
    return pl.pallas_call(
        body,
        out_shape=[jax.ShapeDtypeStruct(s, t) for s, t in outs],
        in_specs=specs or [vmem] * len(args),
        out_specs=[out_spec or vmem] * len(outs),
        scratch_shapes=[pltpu.VMEM(*s) if isinstance(s, tuple) else s for s in scratch],
        cost_estimate=pl.CostEstimate(
            flops=int(8 * n * n * n * units),
            bytes_accessed=4 * n * n * (len(args) + len(outs)),
            transcendentals=0,
        ),
        compiler_params=pltpu.CompilerParams(vmem_limit_bytes=14 << 20),
        input_output_aliases=aliases or {},
    )(*args)


def shards(outer_block, outflow_block, inflow_block, shared_block):
    outer, outflow, inflow, shared = outer_block[0, 0], outflow_block[0, 0], inflow_block[0, 0], shared_block[0, 0]
    n = outer.shape[2]
    half = n // 2
    factor = math.sqrt(n)
    full, part = (2, n, n), (2, n, half)

    shared_r = across(shared, "long", 1)
    inflow_r1 = across(inflow[:, :, half:], "long", 1)
    inflow_r0 = across(inflow[:, :, :half], "long", 1)
    outflow_r = across(outflow, "long", 1)
    cuts = [n * c // 16 for c in [0, 8, 12, 16]]
    outer_rs = [across(outer[:, a:b, :half], "long", 1) for a, b in zip(cuts, cuts[1:])]
    outflow_far = swap(outflow, "short")

    token = pl.pallas_call(
        gate,
        grid=(1,),
        out_shape=jax.ShapeDtypeStruct((1, 16, 128), BF),
        in_specs=[pl.BlockSpec((1, 16, 128), lambda i: (0, 0, 0))],
        out_specs=pl.BlockSpec((1, 16, 128), lambda i: (0, 0, 0)),
        name="gate",
    )(outer)
    product, series, diag = call(
        level_one, [(full, BF)] * 3, (token, shared, shared_r, inflow, outflow, outer), 5, [(full, BF)] * 2
    )
    diag_far = swap(diag, "short")
    series_far = swap(series, "short")
    (product_two,) = call(second_product, [(full, BF)], (diag, diag_far), 1)

    def half_columns(g):
        return call(
            columns,
            [((2,) + part, BF)],
            (shared, shared_r, product, outflow, g, product_two, diag_far, series, series_far),
            5,
            [(part, F32)] + [(part, BF)] * 7,
        )[0]

    xy1 = half_columns(inflow_r1)
    xy1_r = across(xy1, "long", 0)
    xy0 = half_columns(inflow_r0)

    outflow_r_far = swap(outflow_r, "short")
    flag = (lax.axis_index("long") % 2 == 0).astype(jnp.int32).reshape(1)
    hbm = pl.BlockSpec(memory_space=pltpu.HBM)
    smem = pl.BlockSpec(memory_space=pltpu.SMEM)
    (own,) = call(
        functools.partial(last_own, factor),
        [(part, F32)],
        (flag, outflow_r, xy0, outflow, xy1_r, outer),
        0.5,
        [(full, BF), (part, BF), (part, BF), pltpu.SemaphoreType.DMA((3,))],
        [smem] + [hbm] * 5,
    )
    (far,) = call(
        functools.partial(last_far, factor),
        [(part, F32)],
        (flag, outflow_r_far, xy0, outflow_far, xy1_r),
        0.5,
        [(full, BF), (part, BF), pltpu.SemaphoreType.DMA((2,))],
        [smem] + [hbm] * 4,
    )

    def add(first, rows, *more):
        return call(
            functools.partial(finish, factor, first),
            [(part, F32)],
            (own,) + rows + more,
            0,
            [((2,) + rows[0].shape[1:], F32), pltpu.SemaphoreType.DMA((2,))],
            [pl.BlockSpec(memory_space=pltpu.VMEM)] * 2 + [hbm] * len(more),
            hbm,
            {2: 0} if more else None,
        )[0]

    total = ()
    for i, piece in enumerate(outer_rs):
        total = (add(cuts[i], (piece,), *total),)
    own = total[0]
    return own[None], far[None]


def solution(mesh):
    spec = P("short", "long", None, None, None)
    out = P("short", None, None, "long")
    return jax.shard_map(shards, mesh=mesh, in_specs=(spec,) * 4, out_specs=(out, out), check_vma=False)
```
